128 devices in a mesh: ctx: 32 (over x, z, core), exp: 4 (over y).
Axes of the slice: x: 4, y: 4, z: 4, core: 2. Of those that a mesh axis runs over, the one named last changes fastest.
Arguments:
- inputs: bfloat16 [10240, 2048], P(('ctx', 'exp')), may hold values from -6 to 6
- attn_gain: float32 [2048], replicated, may hold values from 0.1 to 1.9
- w_query: bfloat16 [2048, 2048], P(None, 'exp'), as said below
- w_key: bfloat16 [2048, 2048], P(None, 'exp'), as said below
- w_value: bfloat16 [2048, 2048], P(None, 'exp'), may hold values from -0.125 to 0.125
- w_out: bfloat16 [2048, 2048], P('exp'), may hold values from -0.125 to 0.125
- sel_blocks: int32 [10240, 16, 3], P('ctx', 'exp'), may hold values from 0 to 30, as said below
- ffn_gain: float32 [2048], replicated, may hold values from 0.1 to 1.9
- w_gate: bfloat16 [128, 2048, 704], P(('ctx', 'exp')), may hold values from -0.125 to 0.125
- w_up: bfloat16 [128, 2048, 704], P(('ctx', 'exp')), may hold values from -0.125 to 0.125
- w_down: bfloat16 [128, 704, 2048], P(('ctx', 'exp')), may hold values from -0.15625 to 0.15625
- routes: int32 [10240, 6], P(('ctx', 'exp')), may hold values from 0 to 63, all different within a row; in each aligned block of 80 rows (0 to 79, 80 to 159, ...) at most 10 rows name the same one
- gate_weights: float32 [10240, 6], P(('ctx', 'exp')), may hold values from 0.05 to 0.5
Outputs:
- layer_out: bfloat16 [10240, 2048], P(('ctx', 'exp'))
The draws below stay inside these ranges and needn't reach their ends.
Inputs may be any that keep to these rules, and one draw needn't show every extreme that they name: `sel_blocks`: for a query in block b = t // 320, the 3 entries of a head are distinct and lie below max(b, 3); entries below b name selected earlier blocks, and block b - 1 is always among them when b >= 1. `routes`: each row names 6 different experts; within the 80 rows of one device no expert is named by more than 10 rows. `w_query`: entries are bounded in magnitude by 8 * 2048 ** -0.5. `w_key`: entries are bounded in magnitude by 130 * 2048 ** -0.5.
All inputs are finite; a program needn't handle non-finite values.
Results may differ from the reference program's by a relative error of at most 0.014.
Values may be sent and summed in bfloat16 or wider, within the bound.
A program may use at most 128 MiB of HBM per device.

```python
import math
import jax
import jax.numpy as jnp
import numpy as np
from jax import lax

D = 2048
H = 16
HD = 128
FF = 1408
TOPK = 6
SEL = 3
BLOCK = 320
TQ = 80
SEQ = 10240
FH = 704
EXPERTS = 64
CAP = 10


def draw_inputs(key, part):
    key = jax.random.fold_in(key, 11)
    first_key = jax.random.fold_in(key, 0)
    normal_rows = jnp.clip(jax.random.normal(first_key, (SEQ, D), jnp.float32), -6.0, 6.0)
    return (0.5 * normal_rows).astype(jnp.bfloat16)


def query_key(key):
    key = jax.random.fold_in(key, 23)
    first_key, second_key = jax.random.split(key, 2)
    columns = H * HD
    query_weight = jnp.clip(jax.random.normal(first_key, (D, columns), jnp.float32), -5.0, 5.0) * (1.6 / math.sqrt(D))
    other_weight = jnp.clip(jax.random.normal(second_key, (D, columns), jnp.float32), -5.0, 5.0) * (1.6 / math.sqrt(D))
    key_weight = other_weight
    return (query_weight, key_weight)


def draw_w_query(key, part):
    return query_key(key)[0].astype(jnp.bfloat16)


def draw_w_key(key, part):
    return query_key(key)[1].astype(jnp.bfloat16)


def draw_sel_blocks(key, part):
    key = jax.random.fold_in(key, 31)
    block_count = SEQ // BLOCK
    base_score = jax.random.randint(key, (SEQ, H, block_count), 0, 1024)
    own_index = (jnp.arange(SEQ, dtype=jnp.int32) // BLOCK)[:, None, None]
    block_ids = jnp.arange(block_count, dtype=jnp.int32)[None, None, :]
    priority = base_score + jnp.where(block_ids == own_index - 1, 4096, 0) + jnp.where(block_ids == 0, 384, 0)
    priority = jnp.where(block_ids < jnp.maximum(own_index, 3), priority, -1)
    ranked = priority * block_count + block_ids
    _, indices = lax.top_k(ranked, SEL)
    return indices.astype(jnp.int32)


def level_of(own_key, extent, cuts, least, largest):
    def one(axis_at, shards_of):
        draws = jax.random.uniform(jax.random.fold_in(jax.random.fold_in(own_key, 6), axis_at), (shards_of,), jnp.float32, least / len(cuts), largest / len(cuts))
        return jnp.repeat(jnp.exp(draws), extent[axis_at] // shards_of).reshape((-1,) + (1,) * (len(extent) - axis_at - 1))

    factor_of = one(*cuts[0])
    for cut in cuts[1:]:
        factor_of = factor_of * one(*cut)
    return factor_of


def shared_out(stream_key, own, number, rows, count, top, reach, lean):
    order = jax.random.permutation(stream_key, count)
    heavy_load, ordinary = load_shares(count, rows * top, reach, lean, True), load_shares(count, rows * top, reach, lean, False)
    places = jnp.arange(count)

    def named(lengths, rotation):
        used = int((lengths > 0).sum())
        fixed = max(1, used // 4)
        passed = fixed + (places - fixed + rotation * (used - fixed)) % max(1, count - fixed)
        return jnp.zeros((count,), jnp.int32).at[order[jnp.where(places < fixed, places, passed)]].set(jnp.asarray(lengths, jnp.int32))

    lengths = jnp.where(number % 4 == 0, named(heavy_load, number // 4), named(ordinary, number - number // 4 - 1))
    mixed = jax.random.permutation(jax.random.fold_in(own, 3), count)
    source_of, taker = mixed[0:count // 2 * 2:2], mixed[1:count // 2 * 2:2]
    slack = jnp.minimum(lengths[source_of] - 1, reach - lengths[taker]) // 2
    slack = jnp.where((source_of == order[0]) | (taker == order[0]) | (lengths[taker] == 0), 0, jnp.maximum(slack, 0))
    passed = jax.random.randint(jax.random.fold_in(own, 4), (count // 2,), 0, 1 << 20) % (slack + 1)
    lengths = lengths.at[source_of].add(-passed).at[taker].add(passed)
    members = jnp.searchsorted(jnp.cumsum(lengths), jnp.arange(rows * top), side="right").astype(jnp.int32)
    listing = members.reshape(top, rows).T
    listing = listing[jax.random.permutation(jax.random.fold_in(own, 1), rows)]
    rotation = jax.random.randint(jax.random.fold_in(own, 2), (rows, 1), 0, top)
    return jnp.take_along_axis(listing, (jnp.arange(top)[None, :] + rotation) % top, axis=1)


def load_shares(count, total, reach, lean, full):
    loads = [(1 << 20) // math.isqrt(grade ** lean) + 1 for grade in range(1, count + 1)]
    largest = reach if full else min(reach, max(-(-total // count), total * loads[0] // sum(loads)))
    least = 1 if total - largest >= count - 1 else 0
    counts, spare = [largest] + [least] * (count - 1), total - largest - least * (count - 1)
    while spare > 0:
        movable = [i for i in range(1, count) if counts[i] < largest] or [i for i in range(1, count) if counts[i] < reach]
        pool, left = sum([loads[i] for i in movable]), spare
        for i in movable:
            addition = min(reach - counts[i], max(1, left * loads[i] // pool), spare)
            counts[i] = counts[i] + addition
            spare = spare - addition
    return np.array(counts)


def scatter_about(key, extent, spread, limit, pieces=(), kind=jnp.bfloat16):
    drawn = spread * jax.random.normal(key, extent, jnp.float32)
    if pieces:
        drawn = drawn * level_of(key, extent, pieces, -0.22, 0.18)
    return jnp.clip(drawn, -limit, limit).astype(kind)


def setup_inputs(seed: int = 0) -> dict:
    key_list = jax.random.split(jax.random.key(seed), 14)
    inputs = draw_inputs(jax.random.fold_in(key_list[13], 71), 0)
    attn_gain = jnp.clip(1.0 + 0.18 * jax.random.normal(key_list[1], (D,), jnp.float32), 0.1, 1.9)
    w_query = draw_w_query(jax.random.fold_in(key_list[13], 71), 0)
    w_key = draw_w_key(jax.random.fold_in(key_list[13], 71), 0)
    w_value = scatter_about(key_list[4], (D, H * HD), D ** -0.5, 0.125, ((1, 4),))
    w_out = scatter_about(key_list[5], (H * HD, D), (H * HD) ** -0.5, 0.125, ((0, 4),))
    sel_blocks = draw_sel_blocks(jax.random.fold_in(key_list[13], 71), 0)
    ffn_gain = jnp.clip(1.0 + 0.18 * jax.random.normal(key_list[7], (D,), jnp.float32), 0.1, 1.9)
    w_gate = scatter_about(key_list[8], (2 * EXPERTS, D, FH), D ** -0.5, 0.125, ((0, 128),))
    w_up = scatter_about(key_list[9], (2 * EXPERTS, D, FH), D ** -0.5, 0.125, ((0, 128),))
    w_down = scatter_about(key_list[10], (2 * EXPERTS, FH, D), FF ** -0.5, 0.15625, ((0, 128),))
    routes_keys = jax.random.split(jax.random.fold_in(key_list[11], 1), SEQ // TQ)
    routes_turns = jax.random.permutation(jax.random.fold_in(key_list[11], 3), SEQ // TQ)
    routes = jax.vmap(lambda own, number: shared_out(jax.random.fold_in(key_list[11], 2), own, number, TQ, EXPERTS, TOPK, CAP, 2))(routes_keys, routes_turns).reshape((SEQ, TOPK))
    gate_weights = jnp.clip(jnp.exp(math.log(0.5) - 2.3025851 * jax.random.uniform(key_list[12], (SEQ, TOPK), jnp.float32) ** level_of(key_list[12], (SEQ, TOPK), ((0, 128),), -0.2, 0.2)), 0.05, 0.5)
    return dict(inputs=inputs, attn_gain=attn_gain, w_query=w_query, w_key=w_key, w_value=w_value, w_out=w_out, sel_blocks=sel_blocks, ffn_gain=ffn_gain, w_gate=w_gate, w_up=w_up, w_down=w_down, routes=routes, gate_weights=gate_weights)


def normalize(values, gain_vec):
    floats = values.astype(jnp.float32)
    factor = lax.rsqrt(lax.optimization_barrier(jnp.mean(floats * floats, axis=-1, keepdims=True)) + 1e-06)
    return (floats * factor * gain_vec).astype(jnp.bfloat16)

def reference(inputs, attn_gain, w_query, w_key, w_value, w_out, sel_blocks, ffn_gain, w_gate, w_up, w_down, routes, gate_weights):
    block_count = SEQ // BLOCK
    normed = normalize(inputs, attn_gain)

    def project(weight):
        rounded = lax.optimization_barrier(jnp.dot(normed, weight, preferred_element_type=jnp.float32).astype(jnp.bfloat16))
        return rounded.astype(jnp.float32)
    queries = project(w_query).reshape(block_count, BLOCK, H, HD)
    key_rows = project(w_key).reshape(SEQ, H, HD)
    value_rows = project(w_value).reshape(SEQ, H, HD)
    key_pos = jnp.arange(SEQ, dtype=jnp.int32)
    key_block = key_pos // BLOCK
    block_ids = jnp.arange(block_count, dtype=jnp.int32)
    selections = sel_blocks.reshape(block_count, BLOCK, H, SEL)
    scaling = 1.0 / math.sqrt(HD)

    def one_block(operands):
        block_queries, block_sel, block_index = operands
        scores = jnp.einsum('qhd,khd->hqk', block_queries, key_rows) * scaling
        chosen = jnp.any(block_sel[:, :, :, None] == block_ids, axis=2) & (block_ids < block_index)
        picked = jnp.transpose(jnp.take(chosen, key_block, axis=2), (1, 0, 2))
        query_pos = block_index * BLOCK + jnp.arange(BLOCK, dtype=jnp.int32)
        own_block = (key_block[None, :] == block_index) & (key_pos[None, :] <= query_pos[:, None])
        allowed = picked | own_block[None]
        row_max = lax.optimization_barrier(jnp.max(jnp.where(allowed, scores, -jnp.inf), axis=-1, keepdims=True))
        raw_weights = jnp.where(allowed, jnp.exp(scores - row_max), 0.0)
        row_sums = lax.optimization_barrier(jnp.sum(raw_weights, axis=-1))
        rounded = lax.optimization_barrier(raw_weights.astype(jnp.bfloat16)).astype(jnp.float32)
        summed = jnp.einsum('hqk,khd->qhd', rounded, value_rows) / jnp.transpose(row_sums)[:, :, None]
        return summed.astype(jnp.bfloat16).reshape(BLOCK, H * HD)
    attended = lax.map(one_block, (queries, selections, block_ids)).reshape(SEQ, H * HD)
    head_mixed = jnp.dot(attended, w_out, preferred_element_type=jnp.float32)
    residual = (inputs.astype(jnp.float32) + head_mixed).astype(jnp.bfloat16)
    ffn_in = normalize(residual, ffn_gain)
    row_limit = SEQ // TQ * CAP

    def expert_step(running, expert):
        hit = routes == expert
        weight_row = lax.optimization_barrier(jnp.sum(jnp.where(hit, gate_weights, 0.0), axis=1))
        used = jnp.any(hit, axis=1)
        row_index = jnp.nonzero(used, size=row_limit, fill_value=0)[0].astype(jnp.int32)
        valid = jnp.arange(row_limit, dtype=jnp.int32) < jnp.sum(used.astype(jnp.int32))
        chosen_rows = ffn_in[row_index]
        partial_value = jnp.zeros((row_limit, D), jnp.float32)
        for half_index in range(2):
            which_row = 2 * expert + half_index
            gate_part = jnp.dot(chosen_rows, w_gate[which_row], preferred_element_type=jnp.float32)
            up_part = jnp.dot(chosen_rows, w_up[which_row], preferred_element_type=jnp.float32)
            hidden = (jax.nn.silu(gate_part) * up_part).astype(jnp.bfloat16)
            partial_value = partial_value + jnp.dot(hidden, w_down[which_row], preferred_element_type=jnp.float32)
        expert_out = lax.optimization_barrier(partial_value.astype(jnp.bfloat16)).astype(jnp.float32)
        factor = jnp.where(valid, weight_row[row_index], 0.0)
        running = running.at[row_index].add(expert_out * factor[:, None])
        return (running, None)
    expert_mix, _ = lax.scan(expert_step, jnp.zeros((SEQ, D), jnp.float32), jnp.arange(EXPERTS, dtype=jnp.int32))
    return (residual.astype(jnp.float32) + expert_mix).astype(jnp.bfloat16)
```

```python
import functools
import math

import jax
import jax.numpy as jnp
from jax import lax
from jax.experimental import pallas as pl
from jax.experimental.pallas import tpu as pltpu
from jax.sharding import PartitionSpec as P

MESH = pl.DeviceIdType.MESH
NEG = -1e30
LOW = -1e20
TILE = 256


def split_up(value, dim, devices):
    before, after = (value.shape[:dim], value.shape[dim + 1 :])
    return jnp.moveaxis(value.reshape(*before, devices, -1, *after), dim, 0)


def summed_on_arrival(value, axis, dim):
    tiles = split_up(value, dim, lax.axis_size(axis))
    arrived = lax.all_to_all(tiles, axis, split_axis=0, concat_axis=0, tiled=True)
    return arrived.astype(jnp.float32).sum(axis=0)


def items_in_groups(value, axis, split_dim, concat_dim, work, item_dim, out_dim):
    items = jax.tree.leaves(value)[0].shape[item_dim]
    count = 2 if items % 2 == 0 else 1
    finished = []
    for k in range(count):
        group = jax.tree.map(
            lambda a: lax.slice_in_dim(
                a, k * (items // count), (k + 1) * (items // count), axis=item_dim
            ),
            value,
        )
        finished.append(
            work(
                lax.all_to_all(
                    group, axis, split_axis=split_dim, concat_axis=concat_dim, tiled=True
                )
            )
        )
    return jax.tree.map(lambda *parts: jnp.concatenate(parts, axis=out_dim), *finished)


def normalize(values, gain_vec):
    floats = values.astype(jnp.float32)
    factor = lax.rsqrt(jnp.mean(floats * floats, axis=-1, keepdims=True) + 1e-06)
    return (floats * factor * gain_vec).astype(jnp.bfloat16)


def remote(src, dst, send, recv, ctx, exp):
    return pltpu.make_async_remote_copy(
        src_ref=src,
        dst_ref=dst,
        send_sem=send,
        recv_sem=recv,
        device_id=(ctx, exp),
        device_id_type=MESH,
    )


def project_kernel(x_ref, wq, wk, wv, out_ref, rows, wbuf, wsem, lsem, ssem, rsem):
    ctx = lax.axis_index("ctx")
    y = lax.axis_index("exp")
    up, down, far = lax.rem(y + 1, 4), lax.rem(y + 3, 4), lax.rem(y + 2, 4)
    loads = [
        pltpu.make_async_copy(w, wbuf.at[k], wsem.at[k]) for k, w in enumerate((wq, wk, wv))
    ]
    barrier = pltpu.get_barrier_semaphore()
    for peer in (up, down):
        pl.semaphore_signal(barrier, inc=1, device_id=(ctx, peer), device_id_type=MESH)
    pl.semaphore_wait(barrier, 2)
    own = pltpu.make_async_copy(x_ref, rows.at[y], lsem)
    to_up = remote(x_ref, rows.at[y], ssem.at[0], rsem.at[0], ctx, up)
    to_down = remote(x_ref, rows.at[y], ssem.at[1], rsem.at[1], ctx, down)
    to_up.start()
    to_down.start()
    own.start()
    for load in loads:
        load.start()
    half = x_ref.shape[1] // 2
    first, second = pl.ds(0, half), pl.ds(half, half)
    from_down = remote(x_ref, rows.at[down], ssem.at[0], rsem.at[0], ctx, up)
    from_up = remote(x_ref, rows.at[up], ssem.at[1], rsem.at[1], ctx, down)
    from_down.wait_recv()
    on_up = remote(
        rows.at[down, :, first], rows.at[down, :, first], ssem.at[2], rsem.at[2], ctx, up
    )
    on_up.start()
    from_up.wait_recv()
    on_down = remote(
        rows.at[up, :, second], rows.at[up, :, second], ssem.at[3], rsem.at[3], ctx, down
    )
    on_down.start()
    own.wait()
    for load in loads:
        load.wait()
    remote(rows.at[far, :, first], rows.at[far, :, first], ssem.at[2], rsem.at[2], ctx, up).wait_recv()
    remote(
        rows.at[far, :, second], rows.at[far, :, second], ssem.at[3], rsem.at[3], ctx, down
    ).wait_recv()
    block = rows.shape[0] * rows.shape[1]
    for k in range(3):
        for j in range(2):
            part = jnp.dot(
                rows[...].reshape(block, rows.shape[2]),
                wbuf[k, :, j * 256 : (j + 1) * 256],
                preferred_element_type=jnp.float32,
            ).astype(jnp.bfloat16)
            out_ref[2 * j, k * block : (k + 1) * block, :] = part[:, :128]
            out_ref[2 * j + 1, k * block : (k + 1) * block, :] = part[:, 128:]
    to_up.wait_send()
    to_down.wait_send()
    on_up.wait_send()
    on_down.wait_send()


def project(normed, w_query, w_key, w_value):
    rows, width = normed.shape
    cols = w_query.shape[1]
    return pl.pallas_call(
        project_kernel,
        out_shape=jax.ShapeDtypeStruct((cols // 128, 12 * rows, 128), jnp.bfloat16),
        in_specs=[pl.BlockSpec(memory_space=pltpu.VMEM)]
        + [pl.BlockSpec(memory_space=pl.ANY)] * 3,
        out_specs=pl.BlockSpec(memory_space=pltpu.VMEM),
        scratch_shapes=[
            pltpu.VMEM((4, rows, width), jnp.bfloat16),
            pltpu.VMEM((3, width, cols), jnp.bfloat16),
            pltpu.SemaphoreType.DMA((3,)),
            pltpu.SemaphoreType.DMA,
            pltpu.SemaphoreType.DMA((4,)),
            pltpu.SemaphoreType.DMA((4,)),
        ],
        compiler_params=pltpu.CompilerParams(
            collective_id=1, has_side_effects=True, vmem_limit_bytes=48 * 2**20
        ),
        name="project",
    )(normed, w_query, w_key, w_value)


def attend_kernel(
    qkv, sel, att, kv, qs, selb, selq, qt, acc, mrow, lrow, stage,
    xs, xr, zs, zr, fs, fr, ss, sr, os_, or_, lsem,
):
    ctx = lax.axis_index("ctx")
    y = lax.axis_index("exp")
    x, z, c = ctx // 8, lax.rem(ctx // 2, 4), lax.rem(ctx, 2)
    block = att.shape[1]
    cols = 4 * block

    def at(xx, zz, cc):
        return (xx * 4 + zz) * 2 + cc

    def plus(a, b):
        return lax.rem(a + b, 4)

    z_up, z_down, z_far = plus(z, 1), plus(z, 3), plus(z, 2)
    mate = at(x, z, 1 - c)
    barrier = pltpu.get_barrier_semaphore()
    peers = [at(plus(x, d), z, c) for d in (1, 2, 3)] + [at(x, z_up, c), at(x, z_down, c), mate]
    for peer in peers:
        pl.semaphore_signal(barrier, inc=1, device_id=(peer, y), device_id_type=MESH)
    pl.semaphore_wait(barrier, len(peers))

    qpart, kvpart = pl.ds(0, block), pl.ds(block, 2 * block)

    def x_copies(d, source):
        to = plus(x, d)
        return [
            remote(qkv.at[to, kvpart], kv.at[c, z, source], xs.at[0, d], xr.at[0, d], at(to, z, c), y),
            remote(
                qkv.at[to, qpart], qs.at[pl.ds(source * block, block)], xs.at[1, d], xr.at[1, d],
                at(to, z, c), y,
            ),
            remote(sel.at[to], selb.at[source], xs.at[2, d], xr.at[2, d], at(to, z, c), y),
        ]

    def z_copies(src, slot, d):
        return [
            remote(src, slot, zs.at[0, d], zr.at[0, d], at(x, z_up, c), y),
            remote(src, slot, zs.at[1, d], zr.at[1, d], at(x, z_down, c), y),
        ]

    def mate_copy(src, slot, group, d):
        return remote(src, slot, ss.at[group, d], sr.at[group, d], mate, y)

    sent = []

    def go(copy):
        copy.start()
        sent.append(copy)

    mine = qkv.at[x, kvpart]
    for d in (2, 1, 3):
        for copy in x_copies(d, x):
            go(copy)
    for copy in z_copies(mine, kv.at[c, z, x], 0):
        go(copy)
    go(mate_copy(mine, kv.at[c, z, x], 0, 0))
    local = [
        pltpu.make_async_copy(mine, kv.at[c, z, x], lsem.at[0]),
        pltpu.make_async_copy(qkv.at[x, qpart], qs.at[pl.ds(x * block, block)], lsem.at[1]),
        pltpu.make_async_copy(sel.at[x], selb.at[x], lsem.at[2]),
    ]
    for copy in local:
        copy.start()
    mrow[...] = jnp.full_like(mrow, LOW)
    lrow[...] = jnp.zeros_like(lrow)
    acc[...] = jnp.zeros_like(acc)
    for d in (1, 3, 2):
        source = plus(x, 4 - d)
        x_copies(d, source)[0].wait_recv()
        slot = kv.at[c, z, source]
        for copy in z_copies(slot, slot, d):
            go(copy)
        go(mate_copy(slot, slot, 0, d))
    for d in (1, 3, 2):
        for copy in x_copies(d, plus(x, 4 - d))[1:]:
            copy.wait_recv()
    for copy in local:
        copy.wait()
    tiles = cols // TILE
    for t in range(tiles):
        qt[:, t * TILE : (t + 1) * TILE] = qs[t * TILE : (t + 1) * TILE, :].T
    selq[...] = jnp.concatenate([selb[j, :, :block] for j in range(4)], axis=1)

    factor = math.log2(math.e) / math.sqrt(128)
    key_at = lax.broadcasted_iota(jnp.int32, (block, TILE), 0)
    lane = lax.broadcasted_iota(jnp.int32, (1, TILE), 1)
    mine_i = z * 2 + c

    def fold(zk, ck, own):
        group_i = zk * 2 + ck
        active = (mine_i - group_i + 8) // 8

        def over_x(xk, carry):
            keys = kv[ck, zk, xk, :block, :]
            values = kv[ck, zk, xk, block:, :]
            block_id = at(xk, zk, ck).astype(jnp.float32)

            def over_t(t, inner):
                span = pl.ds(pl.multiple_of(t * TILE, TILE), TILE)
                s = jnp.dot(keys, qt[:, span], preferred_element_type=jnp.float32)
                match = (
                    (selq[0:1, span] == block_id)
                    | (selq[1:2, span] == block_id)
                    | (selq[2:3, span] == block_id)
                )
                if own:
                    place = t * TILE + lane - xk * block
                    diagonal = jnp.where((place >= 0) & (place < block), place, -1)
                else:
                    diagonal = jnp.full((1, TILE), -1, jnp.int32)
                last = jnp.where(match, block, diagonal)
                s = jnp.where(key_at <= last, s * factor, NEG)
                old = mrow[0:1, span]
                new = jnp.maximum(old, jnp.max(s, axis=0, keepdims=True))
                p = jnp.exp2(s - new)
                shrink = jnp.exp2(old - new)
                mrow[0:1, span] = new
                lrow[:, span] = lrow[:, span] * shrink + jnp.sum(
                    p.reshape(block // 8, 8, TILE), axis=0
                )
                acc[:, span] = acc[:, span] * shrink + lax.dot_general(
                    values,
                    p.astype(jnp.bfloat16),
                    (((0,), (0,)), ((), ())),
                    preferred_element_type=jnp.float32,
                )
                return inner

            lax.fori_loop((5 * (xk + 1 - active)) // 4, tiles, over_t, 0)
            return carry

        lax.fori_loop(0, 4, over_x, 0)

    def arrived(copies):
        for copy in copies:
            copy.wait_recv()

    fold(z, c, True)
    order = (0, 1, 3, 2)

    def source_of(d):
        return plus(x, 4 - d)

    for d in order:
        for side, (zz, onward, split) in enumerate(((z_down, z_up, (0, 1)), (z_up, z_down, (3, 2)))):
            slot = kv.at[c, zz, source_of(d)]
            z_copies(slot, slot, d)[side].wait_recv()
            if d in split:
                go(remote(slot, slot, fs.at[d], fr.at[d], at(x, onward, c), y))
            go(mate_copy(slot, slot, 1 + side, d))

    def mate_group(group, zz):
        for d in order:
            slot = kv.at[1 - c, zz, source_of(d)]
            mate_copy(slot, slot, group, d).wait_recv()
        fold(zz, 1 - c, False)

    mate_group(0, z)
    fold(z_down, c, False)
    fold(z_up, c, False)
    for d in order:
        slot = kv.at[c, z_far, source_of(d)]
        remote(slot, slot, fs.at[d], fr.at[d], at(x, z_up, c), y).wait_recv()
        go(mate_copy(slot, slot, 3, d))
    mate_group(1, z_down)
    mate_group(2, z_up)
    fold(z_far, c, False)
    mate_group(3, z_far)

    for t in range(tiles):
        span = slice(t * TILE, (t + 1) * TILE)
        total = jnp.sum(lrow[:, span], axis=0, keepdims=True)
        stage[span, :] = (acc[:, span] / total).T.astype(jnp.bfloat16)

    def out_copy(d, source):
        to = plus(x, d)
        return remote(
            stage.at[pl.ds(to * block, block)], att.at[source], os_.at[d], or_.at[d], at(to, z, c), y
        )

    for d in (2, 1, 3):
        go(out_copy(d, x))
    keep = pltpu.make_async_copy(stage.at[pl.ds(x * block, block)], att.at[x], lsem.at[0])
    keep.start()
    for d in (1, 3, 2):
        out_copy(d, plus(x, 4 - d)).wait_recv()
    keep.wait()
    for copy in sent:
        copy.wait_send()


def attend(qkv, sel):
    heads, rows, head_dim = qkv.shape
    block = rows // 3
    cols = 4 * block
    dma = pltpu.SemaphoreType.DMA
    return pl.pallas_call(
        attend_kernel,
        out_shape=jax.ShapeDtypeStruct((heads, block, head_dim), jnp.bfloat16),
        in_specs=[pl.BlockSpec(memory_space=pltpu.VMEM)] * 2,
        out_specs=pl.BlockSpec(memory_space=pltpu.VMEM),
        scratch_shapes=[
            pltpu.VMEM((2, 4, 4, 2 * block, head_dim), jnp.bfloat16),
            pltpu.VMEM((cols, head_dim), jnp.bfloat16),
            pltpu.VMEM((4,) + sel.shape[1:], jnp.float32),
            pltpu.VMEM((8, cols), jnp.float32),
            pltpu.VMEM((head_dim, cols), jnp.bfloat16),
            pltpu.VMEM((head_dim, cols), jnp.float32),
            pltpu.VMEM((8, cols), jnp.float32),
            pltpu.VMEM((8, cols), jnp.float32),
            pltpu.VMEM((cols, head_dim), jnp.bfloat16),
            dma((3, 4)),
            dma((3, 4)),
            dma((2, 4)),
            dma((2, 4)),
            dma((4,)),
            dma((4,)),
            dma((4, 4)),
            dma((4, 4)),
            dma((4,)),
            dma((4,)),
            dma((3,)),
        ],
        compiler_params=pltpu.CompilerParams(
            collective_id=2, has_side_effects=True, vmem_limit_bytes=48 * 2**20
        ),
        name="attend",
    )(qkv, sel)


def shards(
    inputs,
    attn_gain,
    w_query,
    w_key,
    w_value,
    w_out,
    sel_blocks,
    ffn_gain,
    w_gate,
    w_up,
    w_down,
    routes,
    gate_weights,
):
    tok_rows, model_width = inputs.shape
    block_len, heads_here, pick_count = sel_blocks.shape
    ctx_count = lax.axis_size("ctx")
    exp_count = lax.axis_size("exp")
    ctx_index = lax.axis_index("ctx")
    normed = normalize(inputs, attn_gain)
    usable = jnp.where(sel_blocks < ctx_index, sel_blocks, -1).astype(jnp.float32)
    sel = jnp.pad(
        jnp.transpose(usable, (1, 2, 0)),
        ((0, 0), (0, 8 - pick_count), (0, -block_len % 128)),
        constant_values=-1.0,
    )
    qkv = project(normed, w_query, w_key, w_value)
    attended = attend(qkv, sel).transpose(1, 0, 2).reshape(block_len, -1)
    head_mixed = summed_on_arrival(
        jnp.dot(attended, w_out, preferred_element_type=jnp.float32).astype(jnp.bfloat16), "exp", 0
    )
    residual = (inputs.astype(jnp.float32) + head_mixed).astype(jnp.bfloat16)
    ffn_in = normalize(residual, ffn_gain)
    top_count = routes.shape[1]
    experts = ctx_count * exp_count // 2
    capacity = 2 * max(1, (tok_rows * top_count + experts - 1) // experts * 2 // 3)
    flat_routes = routes.reshape(-1)
    expert_ids = jnp.arange(experts, dtype=jnp.int32)
    member = (flat_routes[:, None] == expert_ids[None, :]).astype(jnp.int32)
    before = jnp.cumsum(member, axis=0) - member
    position = jnp.sum(before * member, axis=1)
    slot_index = flat_routes * capacity + position
    slot_ids = jnp.arange(experts * capacity, dtype=jnp.int32)
    placing = jnp.any(
        slot_index.reshape(tok_rows, top_count)[None, :, :] == slot_ids[:, None, None], axis=2
    ).astype(jnp.bfloat16)
    packed = jnp.dot(placing, ffn_in, preferred_element_type=jnp.float32).astype(jnp.bfloat16)

    def expert_pass(arrived):
        sources, slot_count, _ = arrived.shape
        row_data = arrived.reshape(sources * slot_count, model_width)
        gate_part = jnp.dot(row_data, w_gate[0], preferred_element_type=jnp.float32)
        up_part = jnp.dot(row_data, w_up[0], preferred_element_type=jnp.float32)
        hidden = (jax.nn.silu(gate_part) * up_part).astype(jnp.bfloat16)
        partial_value = jnp.dot(hidden, w_down[0], preferred_element_type=jnp.float32).reshape(
            sources, slot_count, model_width
        )
        handed = lax.all_to_all(
            partial_value.astype(jnp.bfloat16),
            ("ctx", "exp"),
            split_axis=0,
            concat_axis=0,
            tiled=True,
        ).astype(partial_value.dtype)
        return handed

    outgoing = jnp.repeat(packed.reshape(experts, capacity, model_width), 2, axis=0)
    returned = items_in_groups(outgoing, ("ctx", "exp"), 0, 0, expert_pass, 1, 1)
    results = returned.reshape(experts, 2, capacity, model_width).sum(axis=1).astype(jnp.bfloat16)
    picked_rows = results.reshape(experts * capacity, model_width)[slot_index].reshape(
        tok_rows, top_count, model_width
    )
    expert_mix = jnp.sum(picked_rows.astype(jnp.float32) * gate_weights[:, :, None], axis=1)
    return (residual.astype(jnp.float32) + expert_mix).astype(jnp.bfloat16)


def solution(mesh):
    placed = (
        P(("ctx", "exp"), None),
        P(),
        P(None, "exp"),
        P(None, "exp"),
        P(None, "exp"),
        P("exp", None),
        P("ctx", "exp", None),
        P(),
        P(("ctx", "exp"), None, None),
        P(("ctx", "exp"), None, None),
        P(("ctx", "exp"), None, None),
        P(("ctx", "exp"), None),
        P(("ctx", "exp"), None),
    )
    return jax.shard_map(
        shards, mesh=mesh, in_specs=placed, out_specs=P(("ctx", "exp"), None), check_vma=False
    )
```
